32 devices in a mesh: row: 16 (over z, y, x), col: 2 (over core).
Axes of the slice: x: 2, y: 2, z: 4, core: 2. Of those that a mesh axis runs over, the one named last changes fastest.
Arguments:
- panel: bfloat16 [4096, 256], P('row', 'col'), may hold values from -0.1875 to 0.1875
- trailing: bfloat16 [4096, 4096], P('row', 'col'), may hold values from -6 to 6
- tile_mask: int32 [16, 16], P('row', 'col'), may hold values 0 or 1
Outputs:
- r_factor: float32 [256, 256], replicated
- coupling: bfloat16 [256, 4096], P(None, 'col')
- updated: bfloat16 [4096, 4096], P('row', 'col')
The draws below stay inside these ranges and needn't reach their ends.
All inputs are finite; a program needn't handle non-finite values. No bound on the sum of `tile_mask` on one device may be relied on, other than what follows from the above.
Results may differ from the reference program's by a relative error of at most 0.0023.
Values may be sent and summed in bfloat16 or wider, within the bound.
No kernel may reach another device: no remote copies, remote signals or barrier semaphores. Data moves between devices by JAX's collectives and lax.ppermute only.
A program may use at most 128 MiB of HBM per device.

```python
import math
import jax
import jax.numpy as jnp
from jax import lax

PANEL = 256
TILE = 256
ROWS = 4096
PARAMS = 4096


def draw_panel(key, part):
    keys = jax.random.split(key, 3)
    base = jnp.clip(jax.random.normal(keys[0], (ROWS, PANEL + 1), jnp.float32), -4.0, 4.0)
    row_scale = jnp.exp(jax.random.uniform(keys[1], (ROWS, 1), jnp.float32, math.log(0.5), math.log(2.0)))
    col_scale = jnp.exp(jax.random.uniform(keys[2], (1, PANEL), jnp.float32, 0.0, math.log(10.0)))
    mixed = base[:, 1:] + 0.9 * base[:, :-1]
    return (jnp.clip(mixed * row_scale * col_scale, -11.9, 11.9) / math.sqrt(ROWS)).astype(jnp.bfloat16)


def plant(drawn, stream_key, least, top_value):
    longest = drawn.shape.index(max(drawn.shape))
    spots = []
    for shift in (0, 1):
        where = [jax.random.randint(jax.random.fold_in(stream_key, axis), (), 0, length) for axis, length in enumerate(drawn.shape)]
        where[longest] = (where[longest] + shift) % drawn.shape[longest]
        spots.append(tuple(where))
    return drawn.at[spots[0]].set(least).at[spots[1]].set(top_value)


def levels(rng, extent, cuts, low, largest):
    level, own = 1.0, jax.random.fold_in(rng, 6)
    for dim, parts in cuts:
        steps = jnp.exp(jax.random.uniform(jax.random.fold_in(own, dim), (parts,), jnp.float32, low / len(cuts), largest / len(cuts)))
        level = level * jnp.repeat(steps, extent[dim] // parts).reshape([-1 if axis == dim else 1 for axis in range(len(extent))])
    return level


def noise(rng, extent, spread, most, pieces=(), kind=jnp.bfloat16):
    entries = spread * jax.random.normal(rng, extent, jnp.float32)
    if pieces:
        entries = entries * levels(rng, extent, pieces, -0.22, 0.18)
    return jnp.clip(entries, -most, most).astype(kind)


def setup_inputs(seed: int = 0) -> dict:
    key_list = jax.random.split(jax.random.key(seed), 4)
    panel = draw_panel(jax.random.fold_in(key_list[3], 71), 0)
    trailing = noise(key_list[1], (ROWS, PARAMS), 1.0, 6.0, ((0, 16), (1, 2)))
    tile_mask = plant((jax.random.randint(key_list[2], (ROWS // TILE, PARAMS // TILE), 0, 4) < 3).astype(jnp.int32), jax.random.fold_in(key_list[2], 1), 0, 1)
    return {"panel": panel, "trailing": trailing, "tile_mask": tile_mask}


damping_total = 0.5

def small_pair(gram):
    order = gram.shape[0]
    places = jnp.arange(order, dtype=jnp.int32)
    rows_list = []
    for index in range(order):
        values = gram[index, :]
        if index > 0:
            done = jnp.stack(rows_list, axis=0)
            values = values - jnp.dot(done[:, index], done, precision=lax.Precision.HIGHEST)
        pivot = jnp.sqrt(values[index])
        rows_list.append(jnp.where(places >= index, values / pivot, jnp.zeros_like(values)))
    factor = jnp.stack(rows_list, axis=0)
    inv_rows = [None] * order
    for index in range(order - 1, -1, -1):
        unit = (places == index).astype(gram.dtype)
        if index < order - 1:
            later = jnp.stack(inv_rows[index + 1:], axis=0)
            unit = unit - jnp.dot(factor[index, index + 1:], later, precision=lax.Precision.HIGHEST)
        inv_rows[index] = unit / factor[index, index]
    return (factor, jnp.stack(inv_rows, axis=0))

def cholesky_pair(gram):
    order = gram.shape[0]
    if order <= 16:
        return small_pair(gram)
    half = order // 2
    upper_a, inverse_a = cholesky_pair(gram[:half, :half])
    upper_b = jnp.dot(inverse_a.T, gram[:half, half:], precision=lax.Precision.HIGHEST)
    schur = gram[half:, half:] - jnp.dot(upper_b.T, upper_b, precision=lax.Precision.HIGHEST)
    upper_c, inverse_c = cholesky_pair(schur)
    inverse_b = -jnp.dot(jnp.dot(inverse_a, upper_b, precision=lax.Precision.HIGHEST), inverse_c, precision=lax.Precision.HIGHEST)
    lower_zero = jnp.zeros((order - half, half), gram.dtype)
    factor = jnp.concatenate([jnp.concatenate([upper_a, upper_b], axis=1), jnp.concatenate([lower_zero, upper_c], axis=1)], axis=0)
    inverse = jnp.concatenate([jnp.concatenate([inverse_a, inverse_b], axis=1), jnp.concatenate([lower_zero, inverse_c], axis=1)], axis=0)
    return (factor, inverse)

def reference(panel, trailing, tile_mask):
    tiles = trailing.reshape(ROWS // TILE, TILE, PARAMS // TILE, TILE)
    masked = (tiles * tile_mask.astype(jnp.bfloat16)[:, None, :, None]).reshape(ROWS, PARAMS)
    gram = lax.dot_general(panel, panel, (((0,), (0,)), ((), ())), preferred_element_type=jnp.float32)
    gram = gram + damping_total * jnp.eye(PANEL, dtype=jnp.float32)
    r_factor, inverse = cholesky_pair(gram)
    basis_t = jnp.dot(inverse.T, panel.astype(jnp.float32).T, precision=lax.Precision.HIGHEST).astype(jnp.bfloat16)
    cross = lax.dot_general(panel, masked, (((0,), (0,)), ((), ())), preferred_element_type=jnp.float32)
    coupling = jnp.dot(inverse.T, cross, precision=lax.Precision.HIGHEST).astype(jnp.bfloat16)
    removed = lax.dot_general(basis_t, coupling, (((0,), (0,)), ((), ())), preferred_element_type=jnp.float32)
    updated = (masked.astype(jnp.float32) - removed).astype(jnp.bfloat16)
    return (r_factor, coupling, updated)
```

```python
import functools

import jax
import jax.numpy as jnp
from jax import lax
from jax.experimental import pallas as pl
from jax.experimental.pallas import tpu as pltpu
from jax.sharding import PartitionSpec as P

TILE = 256
BLOCK = 64
HIGHEST = lax.Precision.HIGHEST


damping_total = 0.5


def inner_product(left, right):
    return lax.dot_general(
        left, right, (((0,), (0,)), ((), ())), preferred_element_type=jnp.float32
    )


def eliminate(groups, base, lane):
    sub = lax.broadcasted_iota(jnp.int32, (8, 1), 0)
    for step in range(0, 8 * len(groups), 2):
        g, r = divmod(step, 8)
        j = base + step
        row0 = groups[g][r : r + 1, :]
        row1 = groups[g][r + 1 : r + 2, :]
        a = row0[:, j : j + 1]
        b = row0[:, j + 1 : j + 2]
        c = row1[:, j + 1 : j + 2]
        inv_a = 1.0 / a
        inv_d = a / (a * c - b * b)
        l = b * inv_a
        at0 = lane == j
        at1 = lane == j + 1
        q0 = (row0 + jnp.where(at0, 1.0, 0.0)) * inv_a
        row1 = jnp.where(at0, -l, row1 - l * row0)
        q1 = (row1 + jnp.where(at1, 1.0, 0.0)) * inv_d
        for i in range(g, len(groups)):
            m0 = groups[i][:, j : j + 1]
            m1 = groups[i][:, j + 1 : j + 2] - l * m0
            if i == g:
                m0 = jnp.where(sub > r, m0, 0.0)
                m1 = jnp.where(sub > r + 1, m1, 0.0)
            groups[i] = groups[i] - m0 * q0 - m1 * q1
    return groups


def factor_kernel(gram_ref, factor_ref, inverse_t_ref, work):
    order = gram_ref.shape[0]
    work[...] = gram_ref[...]
    lane = lax.broadcasted_iota(jnp.int32, (1, order), 1)
    for base in range(0, order, BLOCK):
        end = base + BLOCK
        groups = [work[base + i : base + i + 8, :] for i in range(0, BLOCK, 8)]
        block = jnp.concatenate(eliminate(groups, base, lane), axis=0)
        rows = base + lax.broadcasted_iota(jnp.int32, (BLOCK, order), 0)
        cols = lax.broadcasted_iota(jnp.int32, (BLOCK, order), 1)
        pivots = jnp.sum(jnp.where(rows == cols, block, 0.0), axis=1, keepdims=True)
        scale = lax.rsqrt(pivots)
        scaled = block * scale
        lower = jnp.where(cols < rows, scaled, jnp.where(cols == rows, scale, 0.0))
        factor_ref[base:end, :] = jnp.where(cols >= rows, scaled, 0.0)
        inverse_t_ref[base:end, :] = lower
        if end < order:
            rest = jnp.where((lane >= base) & (lane < end), 0.0, work[end:, :])
            work[end:, :] = rest - lax.dot_general(
                scaled[:, end:],
                jnp.where(cols < end, lower, scaled),
                (((0,), (0,)), ((), ())),
                precision=HIGHEST,
                preferred_element_type=jnp.float32,
            )


def cholesky_pair(gram):
    order = gram.shape[0]
    out = jax.ShapeDtypeStruct((order, order), jnp.float32)
    return pl.pallas_call(
        factor_kernel,
        out_shape=[out, out],
        scratch_shapes=[pltpu.VMEM((order, order), jnp.float32)],
        name="factor",
    )(gram)


def local(panel, trailing, tile_mask):
    gathered = lax.all_gather(panel, "col", axis=1, tiled=True)
    local_rows = trailing.shape[0]
    local_cols = trailing.shape[1]
    tiles = trailing.reshape(local_rows // TILE, TILE, local_cols // TILE, TILE)
    masked = (tiles * tile_mask.astype(jnp.bfloat16)[:, None, :, None]).reshape(
        local_rows, local_cols
    )
    identity = jnp.eye(gathered.shape[1], dtype=jnp.float32)
    gram_local = inner_product(gathered, gathered)
    cross_terms = inner_product(gathered, masked)
    gram_total, summed = lax.psum((gram_local, cross_terms), "row")
    upper_factor, inverse_t = cholesky_pair(gram_total + damping_total * identity)
    coupling = jnp.dot(inverse_t, summed, precision=HIGHEST).astype(jnp.bfloat16)
    basis_t = jnp.dot(
        inverse_t, gathered.astype(jnp.float32).T, precision=HIGHEST
    ).astype(jnp.bfloat16)
    removed = inner_product(basis_t, coupling)
    updated = (masked.astype(jnp.float32) - removed).astype(jnp.bfloat16)
    return (upper_factor, coupling, updated)


def solution(mesh):
    placed = (P("row", "col"), P("row", "col"), P("row", "col"))
    return jax.shard_map(
        local,
        mesh=mesh,
        in_specs=placed,
        out_specs=(P(), P(None, "col"), P("row", "col")),
        check_vma=False,
    )
```

```python
import functools

import jax
import jax.numpy as jnp
from jax import lax
from jax.experimental import pallas as pl
from jax.experimental.pallas import tpu as pltpu
from jax.sharding import PartitionSpec as P

TILE = 256
BLOCK = 64
HIGHEST = lax.Precision.HIGHEST


damping_total = 0.5


def inner_product(left, right):
    return lax.dot_general(
        left, right, (((0,), (0,)), ((), ())), preferred_element_type=jnp.float32
    )


def tree_sum(terms):
    while len(terms) > 1:
        terms = [terms[i] + terms[i + 1] for i in range(0, len(terms), 2)]
    return terms[0]


class Groups:
    def __init__(self, rows, cols):
        self.rows, self.cols = rows, cols
        bits = rows.bit_length() - 1
        self.near = 1 << ((bits + 1) // 2)
        self.far = rows // self.near

    def near_index(self):
        return lax.rem(lax.axis_index("row"), self.near)

    def far_index(self):
        return lax.div(lax.axis_index("row"), self.near)

    def swap(self, value, offset):
        return lax.ppermute(value, "row", [(i, i ^ offset) for i in range(self.rows)])

    def near_swap(self, value, offset):
        return self.swap(value, offset)

    def far_swap(self, value, offset):
        return self.swap(value, offset * self.near)


def eliminate(groups, base, lane):
    sub = lax.broadcasted_iota(jnp.int32, (8, 1), 0)
    for step in range(0, 8 * len(groups), 2):
        g, r = divmod(step, 8)
        j = base + step
        row0 = groups[g][r : r + 1, :]
        row1 = groups[g][r + 1 : r + 2, :]
        a = row0[:, j : j + 1]
        b = row0[:, j + 1 : j + 2]
        c = row1[:, j + 1 : j + 2]
        inv_a = 1.0 / a
        inv_d = a / (a * c - b * b)
        l = b * inv_a
        at0 = lane == j
        at1 = lane == j + 1
        q0 = (row0 + jnp.where(at0, 1.0, 0.0)) * inv_a
        row1 = jnp.where(at0, -l, row1 - l * row0)
        q1 = (row1 + jnp.where(at1, 1.0, 0.0)) * inv_d
        for i in range(g, len(groups)):
            m0 = groups[i][:, j : j + 1]
            m1 = groups[i][:, j + 1 : j + 2] - l * m0
            if i == g:
                m0 = jnp.where(sub > r, m0, 0.0)
                m1 = jnp.where(sub > r + 1, m1, 0.0)
            groups[i] = groups[i] - m0 * q0 - m1 * q1
    return groups


def factor_kernel(own_ref, other_ref, factor_ref, inverse_t_ref, work):
    order = own_ref.shape[0]
    half = order // 2
    side = lax.rem(lax.axis_index("col"), 2)
    work[:, pl.ds(pl.multiple_of(side * half, half), half)] = own_ref[...]
    work[:, pl.ds(pl.multiple_of((1 - side) * half, half), half)] = other_ref[...]
    diagonal = lax.broadcasted_iota(jnp.int32, (order, order), 0) == lax.broadcasted_iota(
        jnp.int32, (order, order), 1
    )
    work[...] += jnp.where(diagonal, damping_total, 0.0)
    lane = lax.broadcasted_iota(jnp.int32, (1, order), 1)
    for base in range(0, order, BLOCK):
        end = base + BLOCK
        groups = [work[base + i : base + i + 8, :] for i in range(0, BLOCK, 8)]
        block = jnp.concatenate(eliminate(groups, base, lane), axis=0)
        rows = base + lax.broadcasted_iota(jnp.int32, (BLOCK, order), 0)
        cols = lax.broadcasted_iota(jnp.int32, (BLOCK, order), 1)
        pivots = jnp.sum(jnp.where(rows == cols, block, 0.0), axis=1, keepdims=True)
        scale = lax.rsqrt(pivots)
        scaled = block * scale
        lower = jnp.where(cols < rows, scaled, jnp.where(cols == rows, scale, 0.0))
        factor_ref[base:end, :] = jnp.where(cols >= rows, scaled, 0.0)
        inverse_t_ref[base:end, :] = lower
        if end < order:
            rest = jnp.where((lane >= base) & (lane < end), 0.0, work[end:, :])
            work[end:, :] = rest - lax.dot_general(
                scaled[:, end:],
                jnp.where(cols < end, lower, scaled),
                (((0,), (0,)), ((), ())),
                precision=HIGHEST,
                preferred_element_type=jnp.float32,
            )


def cholesky_pair(own, other):
    order = own.shape[0]
    out = jax.ShapeDtypeStruct((order, order), jnp.float32)
    return pl.pallas_call(
        factor_kernel,
        out_shape=[out, out],
        scratch_shapes=[pltpu.VMEM((order, order), jnp.float32)],
        cost_estimate=pl.CostEstimate(
            flops=8 * order**3, bytes_accessed=48 * order * order, transcendentals=order
        ),
        name="factor",
    )(own, other)


def gram_kernel(count, *refs):
    out_ref = refs[count]
    half = out_ref.shape[1]
    side = lax.rem(lax.axis_index("col"), 2)
    own = pl.ds(pl.multiple_of(side * half, half), half)
    out_ref[...] = tree_sum(
        [inner_product(ref[...], ref[:, own]) for ref in refs[:count]]
    )


def gram_part(panels):
    order = panels[0].shape[1]
    return pl.pallas_call(
        functools.partial(gram_kernel, len(panels)),
        out_shape=jax.ShapeDtypeStruct((order, order // 2), jnp.float32),
        name="gram_part",
    )(*panels)


def cross_kernel(near, far, *refs):
    panels, tiles, outs = refs[:near], refs[near : 2 * near], refs[2 * near :]
    index = lax.div(lax.axis_index("row"), near)
    width = outs[0].shape[1]
    left = jnp.concatenate([ref[...] for ref in panels], axis=0)
    for k in range(far):
        cols = pl.ds(pl.multiple_of((index ^ k) * width, width), width)
        right = jnp.concatenate([ref[:, cols] for ref in tiles], axis=0)
        outs[k][...] = inner_product(left, right)


def cross_part(groups, panels, tiles):
    width = tiles[0].shape[1] // groups.far
    out = jax.ShapeDtypeStruct((panels[0].shape[1], width), jnp.float32)
    if width % 128:
        whole = inner_product(jnp.concatenate(panels, 0), jnp.concatenate(tiles, 0))
        return [
            lax.dynamic_slice_in_dim(whole, (groups.far_index() ^ k) * width, width, 1)
            for k in range(groups.far)
        ]
    return pl.pallas_call(
        functools.partial(cross_kernel, groups.near, groups.far),
        out_shape=[out] * groups.far,
        name="cross_part",
    )(*panels, *tiles)


def gather_columns(groups, shard):
    near, far = groups.near, groups.far
    width = shard.shape[1]
    wide = jnp.concatenate(
        [shard] + [groups.far_swap(shard, k) for k in range(1, far)], axis=1
    )
    slots = [wide] + [groups.near_swap(wide, k) for k in range(1, near)]
    out = jnp.zeros((shard.shape[0], width * near * far), shard.dtype)
    for i, slot in enumerate(slots):
        for k in range(far):
            start = ((groups.near_index() ^ i) * far + (groups.far_index() ^ k)) * width
            part = slot[:, k * width : (k + 1) * width]
            out = lax.dynamic_update_slice_in_dim(out, part, start, 1)
    return out


def local(groups, panel, trailing, tile_mask):
    near, far = groups.near, groups.far
    gathered = lax.all_gather(panel, "col", axis=1, tiled=True)
    panels = [gathered] + [groups.near_swap(gathered, k) for k in range(1, near)]

    local_rows = trailing.shape[0]
    local_cols = trailing.shape[1]
    tiles = trailing.reshape(local_rows // TILE, TILE, local_cols // TILE, TILE)
    masked = (tiles * tile_mask.astype(jnp.bfloat16)[:, None, :, None]).reshape(
        local_rows, local_cols
    )
    chunk = local_cols // near
    chunks = [
        lax.dynamic_slice_in_dim(masked, (groups.near_index() ^ k) * chunk, chunk, 1)
        for k in range(near)
    ]
    chunks = chunks[:1] + [groups.near_swap(chunks[k], k) for k in range(1, near)]

    gram_terms = gram_part(panels)
    gram_own = tree_sum(
        [gram_terms] + [groups.far_swap(gram_terms, k) for k in range(1, far)]
    )
    gram_other = lax.ppermute(gram_own, "col", [(i, i ^ 1) for i in range(groups.cols)])

    cross_terms = cross_part(groups, panels, chunks)
    summed = tree_sum(
        [cross_terms[0]] + [groups.far_swap(cross_terms[k], k) for k in range(1, far)]
    )

    upper_factor, inverse_t = cholesky_pair(gram_own, gram_other)
    shard = jnp.dot(inverse_t, summed, precision=HIGHEST).astype(jnp.bfloat16)
    coupling = gather_columns(groups, shard)
    basis_t = jnp.dot(
        inverse_t, gathered.astype(jnp.float32).T, precision=HIGHEST
    ).astype(jnp.bfloat16)
    removed = inner_product(basis_t, coupling)
    updated = (masked.astype(jnp.float32) - removed).astype(jnp.bfloat16)
    return (upper_factor, coupling, updated)


def solution(mesh):
    placed = (P("row", "col"), P("row", "col"), P("row", "col"))
    groups = Groups(mesh.shape["row"], mesh.shape["col"])
    return jax.shard_map(
        functools.partial(local, groups),
        mesh=mesh,
        in_specs=placed,
        out_specs=(P(), P(None, "col"), P("row", "col")),
        check_vma=False,
    )
```

```python
import functools

import jax
import jax.numpy as jnp
from jax import lax
from jax.experimental import pallas as pl
from jax.experimental.pallas import tpu as pltpu
from jax.sharding import PartitionSpec as P

TILE = 256
BLOCK = 64
STEP = 8
HIGHEST = lax.Precision.HIGHEST


damping_total = 0.5


def inner_product(left, right):
    return lax.dot_general(
        left, right, (((0,), (0,)), ((), ())), preferred_element_type=jnp.float32
    )


def tree_sum(terms):
    while len(terms) > 1:
        terms = [terms[i] + terms[i + 1] for i in range(0, len(terms), 2)]
    return terms[0]


class Groups:
    def __init__(self, rows, cols):
        self.rows, self.cols = rows, cols
        bits = rows.bit_length() - 1
        self.near = 1 << ((bits + 1) // 2)
        self.far = rows // self.near

    def near_index(self):
        return lax.rem(lax.axis_index("row"), self.near)

    def far_index(self):
        return lax.div(lax.axis_index("row"), self.near)

    def swap(self, value, offset):
        return lax.ppermute(value, "row", [(i, i ^ offset) for i in range(self.rows)])

    def near_swap(self, value, offset):
        return self.swap(value, offset)

    def far_swap(self, value, offset):
        return self.swap(value, offset * self.near)


VMEM = pl.BlockSpec(memory_space=pltpu.VMEM)
PARAMS = pltpu.CompilerParams(vmem_limit_bytes=8 * 2**20)


def spread(value):
    return jnp.broadcast_to(value, (STEP, 128))


def pivot_block(d):
    d = [list(row) for row in d]
    low = [[None] * STEP for _ in range(STEP)]
    inv = [[None] * STEP for _ in range(STEP)]
    pivots, recips = [], []
    for t in range(STEP):
        pivots.append(d[t][t])
        recips.append(1.0 / d[t][t])
        for r in range(t + 1, STEP):
            low[r][t] = d[r][t] * recips[t]
            for s in range(t + 1, r + 1):
                d[r][s] = d[r][s] - low[r][t] * d[s][t]
    for s in range(STEP):
        for r in range(s + 1, STEP):
            total = -low[r][s]
            for t in range(s + 1, r):
                total = total - low[r][t] * inv[t][s]
            inv[r][s] = total
    return pivots, recips, inv


def block_inverse(recips, inv):
    scaled = [[inv[r][s] * recips[r] for s in range(r)] + [recips[r]] for r in range(STEP)]
    out = [[None] * STEP for _ in range(STEP)]
    for s in range(STEP):
        for t in range(s + 1):
            total = scaled[s][t]
            for r in range(s + 1, STEP):
                total = total + inv[r][s] * scaled[r][t]
            out[s][t] = out[t][s] = total
    return out


def weighted(weights, rows):
    total = weights[0] * rows[0]
    for weight, row in zip(weights[1:], rows[1:]):
        total = total + weight * row
    return total


def factor_rows(work, factor_ref, inverse_t_ref, base):
    halves = range(work.shape[1] // 128)
    lane = lax.broadcasted_iota(jnp.int32, (STEP, 128), 1)
    sub = lax.broadcasted_iota(jnp.int32, (STEP, 128), 0)
    steps = range(STEP)
    count = BLOCK // STEP
    rows = [
        [work[base + STEP * i : base + STEP * (i + 1), 128 * h : 128 * (h + 1)] for h in halves]
        for i in range(count)
    ]
    for g in range(count):
        j = base + STEP * g
        home, first = divmod(j, 128)
        columns = [
            [spread(rows[i][home][:, first + s : first + s + 1]) for s in steps]
            for i in range(g, count)
        ]
        block = [[spread(columns[0][s][r : r + 1, :]) for s in range(r + 1)] for r in steps]
        pivots, recips, inv = pivot_block(block)
        own = [[spread(rows[g][h][t : t + 1, :]) for t in steps] for h in halves]

        roots = [lax.rsqrt(pivot) for pivot in pivots]
        scaled_inv = []
        for s in steps:
            column = jnp.where(sub == s, roots[s], 0.0)
            for t in range(s + 1, STEP):
                column = jnp.where(sub == t, inv[t][s] * roots[t], column)
            scaled_inv.append(column)
        corner = jnp.zeros((STEP, 128), jnp.float32)
        for s in steps:
            corner = jnp.where(lane == first + s, scaled_inv[s], corner)
        for h in halves:
            scaled = weighted(scaled_inv, own[h])
            col = lane + 128 * h
            place = (slice(j, j + STEP), slice(128 * h, 128 * (h + 1)))
            factor_ref[place] = jnp.where(col >= j + sub, scaled, 0.0)
            inverse_t_ref[place] = jnp.where(col < j, scaled, corner if h == home else 0.0)

        if g + 1 < count:
            solve = block_inverse(recips, inv)
            pulls = []
            for h in halves:
                pulls.append([weighted(solve[s], own[h]) for s in steps])
                if h == home:
                    for s in steps:
                        for t in steps:
                            entry = solve[s][t] + 1.0 if s == t else solve[s][t]
                            pulls[h][s] = jnp.where(lane == first + t, entry, pulls[h][s])
            for i in range(g + 1, count):
                for h in halves:
                    for s in steps:
                        rows[i][h] = rows[i][h] - columns[i - g][s] * pulls[h][s]


def factor_kernel(own_ref, other_ref, factor_ref, inverse_t_ref, work):
    order = factor_ref.shape[0]
    half = order // 2
    first = lax.rem(lax.axis_index("col"), 2) == 0
    own, other = own_ref[...], other_ref[...]
    packed = jnp.where(first, own, other)
    corner = jnp.where(first, other, own)[:half, :]
    square = packed[:half, :]
    flipped = square.T
    row = lax.broadcasted_iota(jnp.int32, (half, half), 0)
    col = lax.broadcasted_iota(jnp.int32, (half, half), 1)
    damping = jnp.where(row == col, damping_total, 0.0)
    work[:half, :half] = jnp.where(row <= col, square, flipped) + damping
    work[:half, half:] = corner
    work[half:, :half] = corner.T
    last = jnp.where(row == col, packed[half : half + 1, :], jnp.where(row > col, square, flipped))
    work[half:, half:] = last + damping
    for base in range(0, order, BLOCK):
        end = base + BLOCK
        factor_rows(work, factor_ref, inverse_t_ref, base)
        if end < order:
            lane = lax.broadcasted_iota(jnp.int32, (1, order), 1)
            upper = factor_ref[base:end, :]
            rest = jnp.where((lane >= base) & (lane < end), 0.0, work[end:, :])
            work[end:, :] = rest - lax.dot_general(
                upper[:, end:],
                jnp.where(lane < end, inverse_t_ref[base:end, :], upper),
                (((0,), (0,)), ((), ())),
                precision=HIGHEST,
                preferred_element_type=jnp.float32,
            )


def cholesky_pair(own, other):
    order = 2 * own.shape[1]
    out = jax.ShapeDtypeStruct((order, order), jnp.float32)
    return pl.pallas_call(
        factor_kernel,
        out_shape=[out, out],
        in_specs=[VMEM] * 2,
        out_specs=[VMEM] * 2,
        scratch_shapes=[pltpu.VMEM((order, order), jnp.float32)],
        cost_estimate=pl.CostEstimate(
            flops=8 * order**3, bytes_accessed=48 * order * order, transcendentals=order
        ),
        compiler_params=PARAMS,
        name="factor",
    )(own, other)


def gram_kernel(count, panel_ref, out_ref, turned_ref):
    half = out_ref.shape[1]
    rows = panel_ref.shape[0] // count
    grams = []
    for k in range(count):
        part = panel_ref[rows * k : rows * (k + 1), :]
        turned = part.T
        turned_ref[:, rows * k : rows * (k + 1)] = turned
        grams.append(jnp.dot(turned, part, preferred_element_type=jnp.float32))
    gram = tree_sum(grams)
    row = lax.broadcasted_iota(jnp.int32, (half, half), 0)
    col = lax.broadcasted_iota(jnp.int32, (half, half), 1)
    last = gram[half:, half:]
    packed = jnp.where(row <= col, gram[:half, :half], last)
    first = lax.rem(lax.axis_index("col"), 2) == 0
    out_ref[:half, :] = jnp.where(first, packed, gram[:half, half:])
    diagonal = jnp.sum(jnp.where(row == col, last, 0.0), axis=0, keepdims=True)
    out_ref[half:, :] = jnp.broadcast_to(diagonal, (8, half))


def gram_part(count, panel):
    rows, order = panel.shape
    half = order // 2
    return pl.pallas_call(
        functools.partial(gram_kernel, count),
        out_shape=[
            jax.ShapeDtypeStruct((half + 8, half), jnp.float32),
            jax.ShapeDtypeStruct((order, rows), panel.dtype),
        ],
        in_specs=[VMEM],
        out_specs=[VMEM] * 2,
        compiler_params=PARAMS,
        name="gram_part",
    )(panel)


def cross_kernel(near, far, turned_ref, *refs):
    tiles, outs, whole = refs[:near], refs[near : near + far], refs[near + far]
    index = lax.div(lax.axis_index("row"), near)
    width = outs[0].shape[1]
    rows = tiles[0].shape[0]
    total = None
    for k, ref in enumerate(tiles):
        term = jnp.dot(
            turned_ref[:, rows * k : rows * (k + 1)], ref[...], preferred_element_type=jnp.float32
        )
        total = term if total is None else total + term
    whole[...] = total
    for k in range(far):
        start = pl.multiple_of((index ^ k) * width, width)
        outs[k][...] = whole[:, pl.ds(start, width)]


def cross_part(groups, turned, tiles):
    order = turned.shape[0]
    width = tiles[0].shape[1] // groups.far
    if width % 128:
        whole = jnp.dot(
            turned, jnp.concatenate(tiles, 0), preferred_element_type=jnp.float32
        )
        return [
            lax.dynamic_slice_in_dim(whole, (groups.far_index() ^ k) * width, width, 1)
            for k in range(groups.far)
        ]
    return pl.pallas_call(
        functools.partial(cross_kernel, groups.near, groups.far),
        out_shape=[jax.ShapeDtypeStruct((order, width), jnp.float32)] * groups.far,
        in_specs=[VMEM] * (1 + groups.near),
        out_specs=[VMEM] * groups.far,
        scratch_shapes=[pltpu.VMEM((order, tiles[0].shape[1]), jnp.float32)],
        compiler_params=PARAMS,
        name="cross_part",
    )(turned, *tiles)


def update_kernel(near, far, basis_ref, masked_ref, *refs):
    slots, (coupling_ref, updated_ref) = refs[:near], refs[near:]
    index = lax.axis_index("row")
    near_index, far_index = lax.rem(index, near), lax.div(index, near)
    basis = basis_ref[...]
    width = slots[0].shape[1] // far
    for i, slot in enumerate(slots):
        removed = jnp.dot(basis, slot[...], preferred_element_type=jnp.float32)
        for k in range(far):
            start = ((near_index ^ i) * far + (far_index ^ k)) * width
            cols = pl.ds(pl.multiple_of(start, width), width)
            part = slice(k * width, (k + 1) * width)
            coupling_ref[:, cols] = slot[:, part]
            left = masked_ref[:, cols].astype(jnp.float32) - removed[:, part]
            updated_ref[:, cols] = left.astype(updated_ref.dtype)


def update(groups, basis, masked, slots):
    near, far = groups.near, groups.far
    rows, cols = masked.shape
    width = slots[0].shape[1] // far
    if width % 128:
        coupling = jnp.zeros((slots[0].shape[0], cols), slots[0].dtype)
        for i, slot in enumerate(slots):
            for k in range(far):
                start = ((groups.near_index() ^ i) * far + (groups.far_index() ^ k)) * width
                part = slot[:, k * width : (k + 1) * width]
                coupling = lax.dynamic_update_slice_in_dim(coupling, part, start, 1)
        removed = jnp.dot(basis, coupling, preferred_element_type=jnp.float32)
        return coupling, (masked.astype(jnp.float32) - removed).astype(masked.dtype)
    return pl.pallas_call(
        functools.partial(update_kernel, near, far),
        out_shape=[
            jax.ShapeDtypeStruct((slots[0].shape[0], cols), slots[0].dtype),
            jax.ShapeDtypeStruct((rows, cols), masked.dtype),
        ],
        in_specs=[VMEM] * (2 + near),
        out_specs=[VMEM] * 2,
        compiler_params=PARAMS,
        name="update",
    )(basis, masked, *slots)


def gather_slots(groups, shard):
    far = range(1, groups.far)
    wide = jnp.concatenate([shard] + [groups.far_swap(shard, k) for k in far], axis=1)
    return [wide] + [groups.near_swap(wide, k) for k in range(1, groups.near)]


def local(groups, panel, trailing, tile_mask):
    near, far = groups.near, groups.far
    stacked = jnp.concatenate(
        [panel] + [groups.near_swap(panel, k) for k in range(1, near)], axis=0
    )
    gathered = lax.all_gather(stacked, "col", axis=1, tiled=True)

    local_rows = trailing.shape[0]
    local_cols = trailing.shape[1]
    tiles = trailing.reshape(local_rows // TILE, TILE, local_cols // TILE, TILE)
    masked = (tiles * tile_mask.astype(jnp.bfloat16)[:, None, :, None]).reshape(
        local_rows, local_cols
    )
    chunk = local_cols // near
    chunks = [
        lax.dynamic_slice_in_dim(masked, (groups.near_index() ^ k) * chunk, chunk, 1)
        for k in range(near)
    ]
    chunks = chunks[:1] + [groups.near_swap(chunks[k], k) for k in range(1, near)]

    gram_terms, turned = gram_part(near, gathered)
    gram_own = tree_sum(
        [gram_terms] + [groups.far_swap(gram_terms, k) for k in range(1, far)]
    )
    gram_other = lax.ppermute(gram_own, "col", [(i, i ^ 1) for i in range(groups.cols)])

    cross_terms = cross_part(groups, turned, chunks)
    summed = tree_sum(
        [cross_terms[0]] + [groups.far_swap(cross_terms[k], k) for k in range(1, far)]
    )

    upper_factor, inverse_t = cholesky_pair(gram_own, gram_other)
    shard = jnp.dot(inverse_t, summed, precision=HIGHEST).astype(jnp.bfloat16)
    slots = gather_slots(groups, shard)
    basis = lax.dot_general(
        gathered[: panel.shape[0], :].astype(jnp.float32), inverse_t, (((1,), (1,)), ((), ())), precision=HIGHEST
    ).astype(jnp.bfloat16)
    coupling, updated = update(groups, basis, masked, slots)
    return (upper_factor, coupling, updated)


def solution(mesh):
    placed = (P("row", "col"), P("row", "col"), P("row", "col"))
    groups = Groups(mesh.shape["row"], mesh.shape["col"])
    return jax.shard_map(
        functools.partial(local, groups),
        mesh=mesh,
        in_specs=placed,
        out_specs=(P(), P(None, "col"), P("row", "col")),
        check_vma=False,
    )
```

```python
import functools

import jax
import jax.numpy as jnp
from jax import lax
from jax.experimental import pallas as pl
from jax.experimental.pallas import tpu as pltpu
from jax.sharding import PartitionSpec as P

TILE = 256
BLOCK = 128
STEP = 8
HIGHEST = lax.Precision.HIGHEST


damping_total = 0.5


def inner_product(left, right):
    return lax.dot_general(
        left, right, (((0,), (0,)), ((), ())), preferred_element_type=jnp.float32
    )


def tree_sum(terms):
    while len(terms) > 1:
        terms = [terms[i] + terms[i + 1] for i in range(0, len(terms), 2)]
    return terms[0]


class Groups:
    def __init__(self, rows, cols):
        self.rows, self.cols = rows, cols
        bits = rows.bit_length() - 1
        self.near = 1 << ((bits + 1) // 2)
        self.far = rows // self.near

    def near_index(self):
        return lax.rem(lax.axis_index("row"), self.near)

    def far_index(self):
        return lax.div(lax.axis_index("row"), self.near)

    def swap(self, value, offset):
        return lax.ppermute(value, "row", [(i, i ^ offset) for i in range(self.rows)])

    def near_swap(self, value, offset):
        return self.swap(value, offset)

    def far_swap(self, value, offset):
        return self.swap(value, offset * self.near)


VMEM = pl.BlockSpec(memory_space=pltpu.VMEM)
PARAMS = pltpu.CompilerParams(vmem_limit_bytes=8 * 2**20)


def spread(value):
    return jnp.broadcast_to(value, (STEP, 128))


def pivot_block(d):
    d = [list(row) for row in d]
    low = [[None] * STEP for _ in range(STEP)]
    inv = [[None] * STEP for _ in range(STEP)]
    pivots, recips = [], []
    for t in range(0, STEP, 2):
        a, b, c = d[t][t], d[t + 1][t], d[t + 1][t + 1]
        det = a * c - b * b
        recip_a, recip_det = 1.0 / a, 1.0 / det
        pivots += [a, det * recip_a]
        recips += [recip_a, a * recip_det]
        low[t + 1][t] = b * recip_a
        for r in range(t + 2, STEP):
            u, v = d[r][t], d[r][t + 1]
            x, y = c * u - b * v, a * v - b * u
            low[r][t] = u * recip_a
            low[r][t + 1] = y * recip_det
            for s in range(t + 2, r + 1):
                d[r][s] = d[r][s] - (x * d[s][t] + y * d[s][t + 1]) * recip_det
    for s in range(STEP):
        for r in range(s + 1, STEP):
            total = -low[r][s]
            for t in range(s + 1, r):
                total = total - low[r][t] * inv[t][s]
            inv[r][s] = total
    return pivots, recips, inv


def pick(value, index):
    where = jnp.full((STEP, 128), index, jnp.int32)
    return jnp.take_along_axis(value, where, axis=1, mode="promise_in_bounds")


def stack(sub, values):
    out = values[0]
    for i in range(1, STEP):
        out = jnp.where(sub == i, values[i], out)
    return out


def weighted(weights, rows):
    return tree_sum([weight * row for weight, row in zip(weights, rows)])


def factor_rows(work, factor_ref, inverse_t_ref, base):
    halves = range(work.shape[1] // 128)
    lane = lax.broadcasted_iota(jnp.int32, (STEP, 128), 1)
    sub = lax.broadcasted_iota(jnp.int32, (STEP, 128), 0)
    steps = range(STEP)
    count = BLOCK // STEP
    rows = [
        [work[base + STEP * i : base + STEP * (i + 1), 128 * h : 128 * (h + 1)] for h in halves]
        for i in range(count)
    ]
    for g in range(count):
        j = base + STEP * g
        home, first = divmod(j, 128)
        columns = [
            [pick(rows[i][home], first + s) for s in steps]
            for i in range(g, count)
        ]
        block = [[spread(columns[0][s][r : r + 1, :]) for s in range(r + 1)] for r in steps]
        pivots, recips, inv = pivot_block(block)
        own = [[spread(rows[g][h][t : t + 1, :]) for t in steps] for h in halves]

        down = [stack(sub, [inv[t][s] if t > s else float(t == s) for t in steps]) for s in steps]
        across = [stack(sub, [inv[r][s] if r > s else float(r == s) for s in steps]) for r in steps]
        root = lax.rsqrt(stack(sub, pivots))
        corner = jnp.zeros((STEP, 128), jnp.float32)
        for s in steps:
            corner = jnp.where(lane == first + s, down[s], corner)
        solved = [weighted(down, own[h]) for h in halves]
        for h in halves:
            col = lane + 128 * h
            place = (slice(j, j + STEP), slice(128 * h, 128 * (h + 1)))
            edge = corner * root if h == home else 0.0
            factor_ref[place] = jnp.where(col >= j + sub, solved[h] * root, 0.0)
            inverse_t_ref[place] = jnp.where(col < j, solved[h] * root, edge)

        if g + 1 < count:
            inside = (lane >= first) & (lane < first + STEP)
            unit = jnp.where(lane == first + sub, 1.0, 0.0)
            across = [across[r] * recips[r] for r in steps]
            for h in halves:
                full = jnp.where(inside, corner, solved[h]) if h == home else solved[h]
                pull = weighted(across, [spread(full[t : t + 1, :]) for t in steps])
                if h == home:
                    pull = pull + unit
                pulls = [spread(pull[s : s + 1, :]) for s in steps]
                for i in range(g + 1, count):
                    rows[i][h] = rows[i][h] - weighted(columns[i - g], pulls)


def factor_kernel(own_ref, other_ref, factor_ref, inverse_t_ref, work):
    order = factor_ref.shape[0]
    half = order // 2
    first = lax.rem(lax.axis_index("col"), 2) == 0
    own, other = own_ref[...], other_ref[...]
    packed = jnp.where(first, own, other)
    corner = jnp.where(first, other, own)[:half, :]
    square = packed[:half, :]
    flipped = square.T
    row = lax.broadcasted_iota(jnp.int32, (half, half), 0)
    col = lax.broadcasted_iota(jnp.int32, (half, half), 1)
    damping = jnp.where(row == col, damping_total, 0.0)
    work[:half, :half] = jnp.where(row <= col, square, flipped) + damping
    work[:half, half:] = corner
    work[half:, :half] = corner.T
    last = jnp.where(row == col, packed[half : half + 1, :], jnp.where(row > col, square, flipped))
    work[half:, half:] = last + damping
    for base in range(0, order, BLOCK):
        end = base + BLOCK
        factor_rows(work, factor_ref, inverse_t_ref, base)
        if end < order:
            lane = lax.broadcasted_iota(jnp.int32, (1, order), 1)
            upper = factor_ref[base:end, :]
            rest = jnp.where((lane >= base) & (lane < end), 0.0, work[end:, :])
            work[end:, :] = rest - lax.dot_general(
                upper[:, end:],
                jnp.where(lane < end, inverse_t_ref[base:end, :], upper),
                (((0,), (0,)), ((), ())),
                precision=HIGHEST,
                preferred_element_type=jnp.float32,
            )


def cholesky_pair(own, other):
    order = 2 * own.shape[1]
    out = jax.ShapeDtypeStruct((order, order), jnp.float32)
    return pl.pallas_call(
        factor_kernel,
        out_shape=[out, out],
        in_specs=[VMEM] * 2,
        out_specs=[VMEM] * 2,
        scratch_shapes=[pltpu.VMEM((order, order), jnp.float32)],
        cost_estimate=pl.CostEstimate(
            flops=8 * order**3, bytes_accessed=48 * order * order, transcendentals=order
        ),
        compiler_params=PARAMS,
        name="factor",
    )(own, other)


def gram_kernel(count, panel_ref, out_ref, turned_ref):
    half = out_ref.shape[1]
    rows = panel_ref.shape[0] // count
    grams = []
    for k in range(count):
        part = panel_ref[rows * k : rows * (k + 1), :]
        turned = part.T
        turned_ref[:, rows * k : rows * (k + 1)] = turned
        grams.append(jnp.dot(turned, part, preferred_element_type=jnp.float32))
    gram = tree_sum(grams)
    row = lax.broadcasted_iota(jnp.int32, (half, half), 0)
    col = lax.broadcasted_iota(jnp.int32, (half, half), 1)
    last = gram[half:, half:]
    packed = jnp.where(row <= col, gram[:half, :half], last)
    first = lax.rem(lax.axis_index("col"), 2) == 0
    out_ref[:half, :] = jnp.where(first, packed, gram[:half, half:])
    diagonal = jnp.sum(jnp.where(row == col, last, 0.0), axis=0, keepdims=True)
    out_ref[half:, :] = jnp.broadcast_to(diagonal, (8, half))


def gram_part(count, panel):
    rows, order = panel.shape
    half = order // 2
    return pl.pallas_call(
        functools.partial(gram_kernel, count),
        out_shape=[
            jax.ShapeDtypeStruct((half + 8, half), jnp.float32),
            jax.ShapeDtypeStruct((order, rows), panel.dtype),
        ],
        in_specs=[VMEM],
        out_specs=[VMEM] * 2,
        compiler_params=PARAMS,
        name="gram_part",
    )(panel)


def cross_kernel(near, far, turned_ref, *refs):
    tiles, outs, whole = refs[:near], refs[near : near + far], refs[near + far]
    index = lax.div(lax.axis_index("row"), near)
    width = outs[0].shape[1]
    rows = tiles[0].shape[0]
    total = None
    for k, ref in enumerate(tiles):
        term = jnp.dot(
            turned_ref[:, rows * k : rows * (k + 1)], ref[...], preferred_element_type=jnp.float32
        )
        total = term if total is None else total + term
    whole[...] = total
    for k in range(far):
        start = pl.multiple_of((index ^ k) * width, width)
        outs[k][...] = whole[:, pl.ds(start, width)]


def cross_part(groups, turned, tiles):
    order = turned.shape[0]
    width = tiles[0].shape[1] // groups.far
    if width % 128:
        whole = jnp.dot(
            turned, jnp.concatenate(tiles, 0), preferred_element_type=jnp.float32
        )
        return [
            lax.dynamic_slice_in_dim(whole, (groups.far_index() ^ k) * width, width, 1)
            for k in range(groups.far)
        ]
    return pl.pallas_call(
        functools.partial(cross_kernel, groups.near, groups.far),
        out_shape=[jax.ShapeDtypeStruct((order, width), jnp.float32)] * groups.far,
        in_specs=[VMEM] * (1 + groups.near),
        out_specs=[VMEM] * groups.far,
        scratch_shapes=[pltpu.VMEM((order, tiles[0].shape[1]), jnp.float32)],
        compiler_params=PARAMS,
        name="cross_part",
    )(turned, *tiles)


def chunk_kernel(near, mask_hbm, trailing_hbm, *refs):
    outs, (mask, held, sems) = refs[:near], refs[near:]
    index = lax.rem(lax.axis_index("row"), near)
    rows, width = outs[0].shape
    first = pltpu.make_async_copy(mask_hbm, mask, sems.at[near])
    first.start()
    copies = []
    for k in [*range(1, near), 0]:
        cols = pl.ds(pl.multiple_of((index ^ k) * width, width), width)
        copies.append(pltpu.make_async_copy(trailing_hbm.at[:, cols], held.at[k], sems.at[k]))
        copies[-1].start()
    first.wait()
    for k, copy in zip([*range(1, near), 0], copies):
        copy.wait()
        for i in range(rows // TILE):
            for j in range(width // TILE):
                place = (slice(i * TILE, (i + 1) * TILE), slice(j * TILE, (j + 1) * TILE))
                tile = held[(k, *place)]
                present = mask[i, (index ^ k) * (width // TILE) + j] != 0
                outs[k][place] = jnp.where(present, tile, jnp.zeros_like(tile))


def masked_chunks(groups, trailing, tile_mask):
    rows, cols = trailing.shape
    width = cols // groups.near
    out = jax.ShapeDtypeStruct((rows, width), trailing.dtype)
    return pl.pallas_call(
        functools.partial(chunk_kernel, groups.near),
        out_shape=[out] * groups.near,
        in_specs=[pl.BlockSpec(memory_space=pltpu.HBM)] * 2,
        out_specs=[VMEM] * groups.near,
        scratch_shapes=[
            pltpu.SMEM(tile_mask.shape, tile_mask.dtype),
            pltpu.VMEM((groups.near, rows, width), trailing.dtype),
            pltpu.SemaphoreType.DMA((groups.near + 1,)),
        ],
        compiler_params=PARAMS,
        name="chunks",
    )(
        pltpu.with_memory_space_constraint(tile_mask, pltpu.HBM),
        pltpu.with_memory_space_constraint(trailing, pltpu.HBM),
    )


def update_kernel(near, far, basis_ref, *refs):
    chunks, firsts, rests = refs[:near], refs[near : 2 * near], refs[2 * near : 3 * near]
    coupling_ref, updated_ref, work, sems = refs[3 * near :]
    index = lax.axis_index("row")
    near_index, far_index = lax.rem(index, near), lax.div(index, near)
    width = firsts[0].shape[1]
    copies = []

    def send(source, target, cols):
        copy = pltpu.make_async_copy(source, target.at[:, cols], sems.at[len(copies)])
        copy.start()
        copies.append(copy)

    for i in range(near):
        for k in range(far):
            source = firsts[i] if k == 0 else rests[i].at[:, (k - 1) * width : k * width]
            start = ((near_index ^ i) * far + (far_index ^ k)) * width
            send(source, coupling_ref, pl.ds(pl.multiple_of(start, width), width))
    for i in range(near):
        for part in (firsts, rests):
            removed = jnp.dot(basis_ref[...], part[i][...], preferred_element_type=jnp.float32)
            for k in range(part[i].shape[1] // width):
                slot = k if part is firsts else k + 1
                inner = (far_index ^ slot) * width
                left = chunks[i][:, pl.ds(pl.multiple_of(inner, width), width)]
                place = (i * far + slot) * width
                result = left.astype(jnp.float32) - removed[:, k * width : (k + 1) * width]
                work[:, place : place + width] = result.astype(work.dtype)
                start = (near_index ^ i) * far * width + inner
                cols = pl.ds(pl.multiple_of(start, width), width)
                send(work.at[:, place : place + width], updated_ref, cols)
    for copy in copies:
        copy.wait()


def update(groups, basis, chunks, firsts, rests):
    near, far = groups.near, groups.far
    rows, width = chunks[0].shape
    cols = width * near
    dtype = chunks[0].dtype
    if (width // far) % 128:
        return update_plain(groups, basis, chunks, firsts, rests)
    hbm = pl.BlockSpec(memory_space=pltpu.HBM)
    return pl.pallas_call(
        functools.partial(update_kernel, near, far),
        out_shape=[
            jax.ShapeDtypeStruct((firsts[0].shape[0], cols), dtype),
            jax.ShapeDtypeStruct((rows, cols), dtype),
        ],
        in_specs=[VMEM] * (1 + 3 * near),
        out_specs=[hbm] * 2,
        scratch_shapes=[
            pltpu.VMEM((rows, cols), dtype),
            pltpu.SemaphoreType.DMA((2 * near * far,)),
        ],
        compiler_params=PARAMS,
        name="update",
    )(basis, *chunks, *firsts, *rests)


def update_plain(groups, basis, chunks, firsts, rests):
    near, far = groups.near, groups.far
    rows, chunk = chunks[0].shape
    width = firsts[0].shape[1]
    coupling = jnp.zeros((firsts[0].shape[0], chunk * near), firsts[0].dtype)
    masked = jnp.zeros((rows, chunk * near), chunks[0].dtype)
    for i in range(near):
        base = (groups.near_index() ^ i) * chunk
        masked = lax.dynamic_update_slice_in_dim(masked, chunks[i], base, 1)
        slot = jnp.concatenate([firsts[i], rests[i]], axis=1)
        for k in range(far):
            start = base + (groups.far_index() ^ k) * width
            part = slot[:, k * width : (k + 1) * width]
            coupling = lax.dynamic_update_slice_in_dim(coupling, part, start, 1)
    removed = jnp.dot(basis, coupling, preferred_element_type=jnp.float32)
    return coupling, (masked.astype(jnp.float32) - removed).astype(masked.dtype)


def gather_slots(groups, shard):
    near = range(1, groups.near)
    rest = [groups.far_swap(shard, k) for k in range(1, groups.far)]
    rest[1], later = lax.optimization_barrier((rest[1], shard))
    firsts = [shard] + [groups.near_swap(later, k) for k in near]
    rest = jnp.concatenate(rest, axis=1)
    return firsts, [rest] + [groups.near_swap(rest, k) for k in near]


def local(groups, panel, trailing, tile_mask):
    near, far = groups.near, groups.far
    stacked = jnp.concatenate(
        [panel] + [groups.near_swap(panel, k) for k in range(1, near)], axis=0
    )
    gathered = lax.all_gather(stacked, "col", axis=1, tiled=True)

    chunks = masked_chunks(groups, trailing, tile_mask)
    tiles = [chunks[0]] + [groups.near_swap(chunks[k], k) for k in range(1, near)]

    gram_terms, turned = gram_part(near, gathered)
    gram_own = tree_sum(
        [gram_terms] + [groups.far_swap(gram_terms, k) for k in range(1, far)]
    )
    gram_other = lax.ppermute(gram_own, "col", [(i, i ^ 1) for i in range(groups.cols)])

    cross_terms = cross_part(groups, turned, tiles)
    summed = tree_sum(
        [cross_terms[0]] + [groups.far_swap(cross_terms[k], k) for k in range(1, far)]
    )

    upper_factor, inverse_t = cholesky_pair(gram_own, gram_other)
    shard = jnp.dot(inverse_t, summed, precision=HIGHEST).astype(jnp.bfloat16)
    firsts, rests = gather_slots(groups, shard)
    rows = gathered[: panel.shape[0], :].astype(jnp.float32)
    basis = lax.dot_general(
        rows, inverse_t, (((1,), (1,)), ((), ())), precision=HIGHEST
    ).astype(jnp.bfloat16)
    coupling, updated = update(groups, basis, chunks, firsts, rests)
    return (upper_factor, coupling, updated)


def solution(mesh):
    placed = (P("row", "col"), P("row", "col"), P("row", "col"))
    groups = Groups(mesh.shape["row"], mesh.shape["col"])
    return jax.shard_map(
        functools.partial(local, groups),
        mesh=mesh,
        in_specs=placed,
        out_specs=(P(), P(None, "col"), P("row", "col")),
        check_vma=False,
    )
```

```python
import functools

import jax
import jax.numpy as jnp
from jax import lax
from jax.experimental import pallas as pl
from jax.experimental.pallas import tpu as pltpu
from jax.sharding import PartitionSpec as P

TILE = 256
BLOCK = 128
STEP = 8
HIGHEST = lax.Precision.HIGHEST


damping_total = 0.5


def inner_product(left, right):
    return lax.dot_general(
        left, right, (((0,), (0,)), ((), ())), preferred_element_type=jnp.float32
    )


def tree_sum(terms):
    while len(terms) > 1:
        terms = [terms[i] + terms[i + 1] for i in range(0, len(terms), 2)]
    return terms[0]


class Groups:
    def __init__(self, rows, cols):
        self.rows, self.cols = rows, cols
        bits = rows.bit_length() - 1
        self.near = 1 << ((bits + 1) // 2)
        self.far = rows // self.near

    def near_index(self):
        return lax.rem(lax.axis_index("row"), self.near)

    def far_index(self):
        return lax.div(lax.axis_index("row"), self.near)

    def swap(self, value, offset):
        return lax.ppermute(value, "row", [(i, i ^ offset) for i in range(self.rows)])

    def near_swap(self, value, offset):
        return self.swap(value, offset)

    def far_swap(self, value, offset):
        return self.swap(value, offset * self.near)


VMEM = pl.BlockSpec(memory_space=pltpu.VMEM)
PARAMS = pltpu.CompilerParams(vmem_limit_bytes=8 * 2**20)


def spread(value):
    return jnp.broadcast_to(value, (STEP, 128))


def pivot_block(d):
    d = [list(row) for row in d]
    low = [[None] * STEP for _ in range(STEP)]
    inv = [[None] * STEP for _ in range(STEP)]
    pivots, recips = [], []
    for t in range(0, STEP, 2):
        a, b, c = d[t][t], d[t + 1][t], d[t + 1][t + 1]
        det = a * c - b * b
        recip_a, recip_det = 1.0 / a, 1.0 / det
        pivots += [a, det * recip_a]
        recips += [recip_a, a * recip_det]
        low[t + 1][t] = b * recip_a
        for r in range(t + 2, STEP):
            u, v = d[r][t], d[r][t + 1]
            x, y = c * u - b * v, a * v - b * u
            low[r][t] = u * recip_a
            low[r][t + 1] = y * recip_det
            for s in range(t + 2, r + 1):
                d[r][s] = d[r][s] - (x * d[s][t] + y * d[s][t + 1]) * recip_det
    for s in range(STEP):
        for r in range(s + 1, STEP):
            total = -low[r][s]
            for t in range(s + 1, r):
                total = total - low[r][t] * inv[t][s]
            inv[r][s] = total
    return pivots, recips, inv


def pick(value, index):
    where = jnp.full((STEP, 128), index, jnp.int32)
    return jnp.take_along_axis(value, where, axis=1, mode="promise_in_bounds")


def stack(sub, values):
    out = values[0]
    for i in range(1, STEP):
        out = jnp.where(sub == i, values[i], out)
    return out


def weighted(weights, rows):
    return tree_sum([weight * row for weight, row in zip(weights, rows)])


def factor_rows(work, factor_ref, inverse_t_ref, base):
    halves = range(work.shape[1] // 128)
    lane = lax.broadcasted_iota(jnp.int32, (STEP, 128), 1)
    sub = lax.broadcasted_iota(jnp.int32, (STEP, 128), 0)
    steps = range(STEP)
    count = BLOCK // STEP
    rows = [
        [work[base + STEP * i : base + STEP * (i + 1), 128 * h : 128 * (h + 1)] for h in halves]
        for i in range(count)
    ]
    for g in range(count):
        j = base + STEP * g
        home, first = divmod(j, 128)
        columns = [
            [pick(rows[i][home], first + s) for s in steps]
            for i in range(g, count)
        ]
        block = [[spread(columns[0][s][r : r + 1, :]) for s in range(r + 1)] for r in steps]
        pivots, recips, inv = pivot_block(block)
        own = [[spread(rows[g][h][t : t + 1, :]) for t in steps] for h in halves]

        down = [stack(sub, [inv[t][s] if t > s else float(t == s) for t in steps]) for s in steps]
        across = [stack(sub, [inv[r][s] if r > s else float(r == s) for s in steps]) for r in steps]
        root = lax.rsqrt(stack(sub, pivots))
        corner = jnp.zeros((STEP, 128), jnp.float32)
        for s in steps:
            corner = jnp.where(lane == first + s, down[s], corner)
        solved = [weighted(down, own[h]) for h in halves]
        for h in halves:
            col = lane + 128 * h
            place = (slice(j, j + STEP), slice(128 * h, 128 * (h + 1)))
            edge = corner * root if h == home else 0.0
            factor_ref[place] = jnp.where(col >= j + sub, solved[h] * root, 0.0)
            inverse_t_ref[place] = jnp.where(col < j, solved[h] * root, edge)

        if g + 1 < count:
            inside = (lane >= first) & (lane < first + STEP)
            unit = jnp.where(lane == first + sub, 1.0, 0.0)
            across = [across[r] * recips[r] for r in steps]
            for h in halves:
                full = jnp.where(inside, corner, solved[h]) if h == home else solved[h]
                pull = weighted(across, [spread(full[t : t + 1, :]) for t in steps])
                if h == home:
                    pull = pull + unit
                pulls = [spread(pull[s : s + 1, :]) for s in steps]
                for i in range(g + 1, count):
                    rows[i][h] = rows[i][h] - weighted(columns[i - g], pulls)


def factor_kernel(own_ref, other_ref, factor_ref, inverse_t_ref, work):
    order = factor_ref.shape[0]
    half = order // 2
    first = lax.rem(lax.axis_index("col"), 2) == 0
    own, other = own_ref[...], other_ref[...]
    packed = jnp.where(first, own, other)
    corner = jnp.where(first, other, own)[:half, :]
    square = packed[:half, :]
    flipped = square.T
    row = lax.broadcasted_iota(jnp.int32, (half, half), 0)
    col = lax.broadcasted_iota(jnp.int32, (half, half), 1)
    damping = jnp.where(row == col, damping_total, 0.0)
    work[:half, :half] = jnp.where(row <= col, square, flipped) + damping
    work[:half, half:] = corner
    work[half:, :half] = corner.T
    last = jnp.where(row == col, packed[half : half + 1, :], jnp.where(row > col, square, flipped))
    work[half:, half:] = last + damping
    for base in range(0, order, BLOCK):
        end = base + BLOCK
        factor_rows(work, factor_ref, inverse_t_ref, base)
        if end < order:
            lane = lax.broadcasted_iota(jnp.int32, (1, order), 1)
            upper = factor_ref[base:end, :]
            rest = jnp.where((lane >= base) & (lane < end), 0.0, work[end:, :])
            work[end:, :] = rest - lax.dot_general(
                upper[:, end:],
                jnp.where(lane < end, inverse_t_ref[base:end, :], upper),
                (((0,), (0,)), ((), ())),
                precision=HIGHEST,
                preferred_element_type=jnp.float32,
            )


def cholesky_pair(own, other):
    order = 2 * own.shape[1]
    out = jax.ShapeDtypeStruct((order, order), jnp.float32)
    return pl.pallas_call(
        factor_kernel,
        out_shape=[out, out],
        in_specs=[VMEM] * 2,
        out_specs=[VMEM] * 2,
        scratch_shapes=[pltpu.VMEM((order, order), jnp.float32)],
        cost_estimate=pl.CostEstimate(
            flops=8 * order**3, bytes_accessed=48 * order * order, transcendentals=order
        ),
        compiler_params=PARAMS,
        name="factor",
    )(own, other)


def gram_kernel(count, panel_ref, out_ref, turned_ref):
    half = out_ref.shape[1]
    rows = panel_ref.shape[0] // count
    grams = []
    for k in range(count):
        part = panel_ref[rows * k : rows * (k + 1), :]
        turned = part.T
        turned_ref[:, rows * k : rows * (k + 1)] = turned
        grams.append(jnp.dot(turned, part, preferred_element_type=jnp.float32))
    gram = tree_sum(grams)
    row = lax.broadcasted_iota(jnp.int32, (half, half), 0)
    col = lax.broadcasted_iota(jnp.int32, (half, half), 1)
    last = gram[half:, half:]
    packed = jnp.where(row <= col, gram[:half, :half], last)
    first = lax.rem(lax.axis_index("col"), 2) == 0
    out_ref[:half, :] = jnp.where(first, packed, gram[:half, half:])
    diagonal = jnp.sum(jnp.where(row == col, last, 0.0), axis=0, keepdims=True)
    out_ref[half:, :] = jnp.broadcast_to(diagonal, (8, half))


def gram_part(count, panel):
    rows, order = panel.shape
    half = order // 2
    return pl.pallas_call(
        functools.partial(gram_kernel, count),
        out_shape=[
            jax.ShapeDtypeStruct((half + 8, half), jnp.float32),
            jax.ShapeDtypeStruct((order, rows), panel.dtype),
        ],
        in_specs=[VMEM],
        out_specs=[VMEM] * 2,
        compiler_params=PARAMS,
        name="gram_part",
    )(panel)


def cross_kernel(near, far, turned_ref, *refs):
    tiles, outs, whole = refs[:near], refs[near : near + far], refs[near + far]
    index = lax.div(lax.axis_index("row"), near)
    width = outs[0].shape[1]
    rows = tiles[0].shape[0]
    total = None
    for k, ref in enumerate(tiles):
        term = jnp.dot(
            turned_ref[:, rows * k : rows * (k + 1)], ref[...], preferred_element_type=jnp.float32
        )
        total = term if total is None else total + term
    whole[...] = total
    for k in range(far):
        start = pl.multiple_of((index ^ k) * width, width)
        outs[k][...] = whole[:, pl.ds(start, width)]


def cross_part(groups, turned, tiles):
    order = turned.shape[0]
    width = tiles[0].shape[1] // groups.far
    if width % 128:
        whole = jnp.dot(
            turned, jnp.concatenate(tiles, 0), preferred_element_type=jnp.float32
        )
        return [
            lax.dynamic_slice_in_dim(whole, (groups.far_index() ^ k) * width, width, 1)
            for k in range(groups.far)
        ]
    return pl.pallas_call(
        functools.partial(cross_kernel, groups.near, groups.far),
        out_shape=[jax.ShapeDtypeStruct((order, width), jnp.float32)] * groups.far,
        in_specs=[VMEM] * (1 + groups.near),
        out_specs=[VMEM] * groups.far,
        scratch_shapes=[pltpu.VMEM((order, tiles[0].shape[1]), jnp.float32)],
        compiler_params=PARAMS,
        name="cross_part",
    )(turned, *tiles)


def chunk_kernel(near, mask_hbm, trailing_hbm, *refs):
    outs, (mask, held, sems) = refs[:near], refs[near:]
    index = lax.rem(lax.axis_index("row"), near)
    rows, width = outs[0].shape
    first = pltpu.make_async_copy(mask_hbm, mask, sems.at[near])
    first.start()
    copies = []
    for k in [*range(1, near), 0]:
        cols = pl.ds(pl.multiple_of((index ^ k) * width, width), width)
        copies.append(pltpu.make_async_copy(trailing_hbm.at[:, cols], held.at[k], sems.at[k]))
        copies[-1].start()
    first.wait()
    for k, copy in zip([*range(1, near), 0], copies):
        copy.wait()
        for i in range(rows // TILE):
            for j in range(width // TILE):
                place = (slice(i * TILE, (i + 1) * TILE), slice(j * TILE, (j + 1) * TILE))
                tile = held[(k, *place)]
                present = mask[i, (index ^ k) * (width // TILE) + j] != 0
                outs[k][place] = jnp.where(present, tile, jnp.zeros_like(tile))


def masked_chunks(groups, trailing, tile_mask):
    rows, cols = trailing.shape
    width = cols // groups.near
    out = jax.ShapeDtypeStruct((rows, width), trailing.dtype)
    return pl.pallas_call(
        functools.partial(chunk_kernel, groups.near),
        out_shape=[out] * groups.near,
        in_specs=[pl.BlockSpec(memory_space=pltpu.HBM)] * 2,
        out_specs=[VMEM] * groups.near,
        scratch_shapes=[
            pltpu.SMEM(tile_mask.shape, tile_mask.dtype),
            pltpu.VMEM((groups.near, rows, width), trailing.dtype),
            pltpu.SemaphoreType.DMA((groups.near + 1,)),
        ],
        compiler_params=PARAMS,
        name="chunks",
    )(
        pltpu.with_memory_space_constraint(tile_mask, pltpu.HBM),
        pltpu.with_memory_space_constraint(trailing, pltpu.HBM),
    )


def update_kernel(near, far, held, basis_ref, *refs):
    count = len(held)
    chunks, parts = refs[:count], refs[count : 2 * count]
    coupling_ref, updated_ref, work, sems = refs[-4:]
    index = lax.axis_index("row")
    near_index, far_index = lax.rem(index, near), lax.div(index, near)
    copies = []

    def send(source, target, cols):
        copy = pltpu.make_async_copy(source, target.at[:, cols], sems.at[len(copies)])
        copy.start()
        copies.append(copy)

    place = 0
    for (offset, slots), chunk, part in zip(held, chunks, parts):
        width = part.shape[1] // len(slots)
        for k, slot in enumerate(slots):
            start = ((near_index ^ offset) * far + (far_index ^ slot)) * width
            cols = pl.ds(pl.multiple_of(start, width), width)
            send(part.at[:, k * width : (k + 1) * width], coupling_ref, cols)
    for (offset, slots), chunk, part in zip(held, chunks, parts):
        width = part.shape[1] // len(slots)
        removed = jnp.dot(basis_ref[...], part[...], preferred_element_type=jnp.float32)
        for k, slot in enumerate(slots):
            inner = (far_index ^ slot) * width
            left = chunk[:, pl.ds(pl.multiple_of(inner, width), width)].astype(jnp.float32)
            result = left - removed[:, k * width : (k + 1) * width]
            work[:, place : place + width] = result.astype(work.dtype)
            start = (near_index ^ offset) * far * width + inner
            cols = pl.ds(pl.multiple_of(start, width), width)
            send(work.at[:, place : place + width], updated_ref, cols)
            place += width
    for copy in copies:
        copy.wait()


def update_part(groups, basis, chunks, held, parts, outs):
    near, far = groups.near, groups.far
    rows, chunk = chunks[0].shape
    cols = chunk * near
    pieces = sum(len(slots) for _, slots in held)
    dtype = chunks[0].dtype
    count = 1 + 2 * len(held)
    hbm = pl.BlockSpec(memory_space=pltpu.HBM)
    return pl.pallas_call(
        functools.partial(update_kernel, near, far, held),
        out_shape=[
            jax.ShapeDtypeStruct((parts[0].shape[0], cols), dtype),
            jax.ShapeDtypeStruct((rows, cols), dtype),
        ],
        in_specs=[VMEM] * count + [hbm] * len(outs),
        out_specs=[hbm] * 2,
        input_output_aliases={count + i: i for i in range(len(outs))},
        scratch_shapes=[
            pltpu.VMEM((rows, pieces * (chunk // far)), dtype),
            pltpu.SemaphoreType.DMA((2 * pieces,)),
        ],
        compiler_params=PARAMS,
        cost_estimate=pl.CostEstimate(
            flops=2 * rows * parts[0].shape[0] * pieces * (chunk // far),
            bytes_accessed=16 * rows * pieces * (chunk // far),
            transcendentals=0,
        ),
        name="update",
    )(basis, *[chunks[offset] for offset, _ in held], *parts, *outs)


def update(groups, basis, chunks, firsts, rests):
    near = groups.near
    if (chunks[0].shape[1] // groups.far) % 128:
        return update_plain(groups, basis, chunks, firsts, rests)
    early, late = far_slots(groups)
    held = [(0, early), (0, late)] + [(i, early) for i in range(1, near)]
    outs = update_part(groups, basis, chunks, held, [firsts[0], rests[0], *firsts[1:]], [])
    held = [(i, late) for i in range(1, near)]
    return update_part(groups, basis, chunks, held, rests[1:], outs)


def update_plain(groups, basis, chunks, firsts, rests):
    near, far = groups.near, groups.far
    rows, chunk = chunks[0].shape
    width = chunk // far
    early, late = far_slots(groups)
    coupling = jnp.zeros((firsts[0].shape[0], chunk * near), firsts[0].dtype)
    masked = jnp.zeros((rows, chunk * near), chunks[0].dtype)
    for i in range(near):
        base = (groups.near_index() ^ i) * chunk
        masked = lax.dynamic_update_slice_in_dim(masked, chunks[i], base, 1)
        slots = jnp.concatenate([firsts[i], rests[i]], axis=1)
        for k, slot in enumerate([*early, *late]):
            start = base + (groups.far_index() ^ slot) * width
            part = slots[:, k * width : (k + 1) * width]
            coupling = lax.dynamic_update_slice_in_dim(coupling, part, start, 1)
    removed = jnp.dot(basis, coupling, preferred_element_type=jnp.float32)
    return coupling, (masked.astype(jnp.float32) - removed).astype(masked.dtype)


def far_slots(groups):
    return [0], list(range(1, groups.far))


def gather_slots(groups, shard):
    near = range(1, groups.near)
    rest = [groups.far_swap(shard, k) for k in range(1, groups.far)]
    rest[1], later = lax.optimization_barrier((rest[1], shard))
    firsts = [shard] + [groups.near_swap(later, k) for k in near]
    rest = jnp.concatenate(rest, axis=1)
    return firsts, [rest] + [groups.near_swap(rest, k) for k in near]


def local(groups, panel, trailing, tile_mask):
    near, far = groups.near, groups.far
    stacked = jnp.concatenate(
        [panel] + [groups.near_swap(panel, k) for k in range(1, near)], axis=0
    )
    gathered = lax.all_gather(stacked, "col", axis=1, tiled=True)

    chunks = masked_chunks(groups, trailing, tile_mask)
    tiles = [chunks[0]] + [groups.near_swap(chunks[k], k) for k in range(1, near)]

    gram_terms, turned = gram_part(near, gathered)
    gram_own = tree_sum(
        [gram_terms] + [groups.far_swap(gram_terms, k) for k in range(1, far)]
    )
    gram_other = lax.ppermute(gram_own, "col", [(i, i ^ 1) for i in range(groups.cols)])

    cross_terms = cross_part(groups, turned, tiles)
    summed = tree_sum(
        [cross_terms[0]] + [groups.far_swap(cross_terms[k], k) for k in range(1, far)]
    )

    upper_factor, inverse_t = cholesky_pair(gram_own, gram_other)
    shard = jnp.dot(inverse_t, summed, precision=HIGHEST).astype(jnp.bfloat16)
    firsts, rests = gather_slots(groups, shard)
    rows = gathered[: panel.shape[0], :].astype(jnp.float32)
    basis = lax.dot_general(
        rows, inverse_t, (((1,), (1,)), ((), ())), precision=HIGHEST
    ).astype(jnp.bfloat16)
    coupling, updated = update(groups, basis, chunks, firsts, rests)
    return (upper_factor, coupling, updated)


def solution(mesh):
    placed = (P("row", "col"), P("row", "col"), P("row", "col"))
    groups = Groups(mesh.shape["row"], mesh.shape["col"])
    return jax.shard_map(
        functools.partial(local, groups),
        mesh=mesh,
        in_specs=placed,
        out_specs=(P(), P(None, "col"), P("row", "col")),
        check_vma=False,
    )
```

```python
import functools

import jax
import jax.numpy as jnp
from jax import lax
from jax.experimental import pallas as pl
from jax.experimental.pallas import tpu as pltpu
from jax.sharding import PartitionSpec as P

TILE = 256
BLOCK = 128
STEP = 8
HIGHEST = lax.Precision.HIGHEST


damping_total = 0.5


def inner_product(left, right):
    return lax.dot_general(
        left, right, (((0,), (0,)), ((), ())), preferred_element_type=jnp.float32
    )


def tree_sum(terms):
    while len(terms) > 1:
        terms = [terms[i] + terms[i + 1] for i in range(0, len(terms), 2)]
    return terms[0]


class Groups:
    def __init__(self, rows, cols):
        self.rows, self.cols = rows, cols
        bits = rows.bit_length() - 1
        self.near = 1 << ((bits + 1) // 2)
        self.far = rows // self.near

    def near_index(self):
        return lax.rem(lax.axis_index("row"), self.near)

    def far_index(self):
        return lax.div(lax.axis_index("row"), self.near)

    def swap(self, value, offset):
        return lax.ppermute(value, "row", [(i, i ^ offset) for i in range(self.rows)])

    def near_swap(self, value, offset):
        return self.swap(value, offset)

    def far_swap(self, value, offset):
        return self.swap(value, offset * self.near)


VMEM = pl.BlockSpec(memory_space=pltpu.VMEM)
PARAMS = pltpu.CompilerParams(vmem_limit_bytes=8 * 2**20)


def spread(value):
    return jnp.broadcast_to(value, (STEP, 128))


def pivot_block(d):
    d = [list(row) for row in d]
    low = [[None] * STEP for _ in range(STEP)]
    inv = [[None] * STEP for _ in range(STEP)]
    pivots, recips = [], []
    for t in range(0, STEP, 2):
        a, b, c = d[t][t], d[t + 1][t], d[t + 1][t + 1]
        det = a * c - b * b
        recip_a, recip_det = 1.0 / a, 1.0 / det
        pivots += [a, det * recip_a]
        recips += [recip_a, a * recip_det]
        low[t + 1][t] = b * recip_a
        for r in range(t + 2, STEP):
            u, v = d[r][t], d[r][t + 1]
            x, y = c * u - b * v, a * v - b * u
            low[r][t] = u * recip_a
            low[r][t + 1] = y * recip_det
            for s in range(t + 2, r + 1):
                d[r][s] = d[r][s] - (x * d[s][t] + y * d[s][t + 1]) * recip_det
    for s in range(STEP):
        for r in range(s + 1, STEP):
            total = -low[r][s]
            for t in range(s + 1, r):
                total = total - low[r][t] * inv[t][s]
            inv[r][s] = total
    return pivots, recips, inv


def pick(value, index):
    where = jnp.full((STEP, 128), index, jnp.int32)
    return jnp.take_along_axis(value, where, axis=1, mode="promise_in_bounds")


def stack(sub, values):
    out = values[0]
    for i in range(1, STEP):
        out = jnp.where(sub == i, values[i], out)
    return out


def weighted(weights, rows):
    return tree_sum([weight * row for weight, row in zip(weights, rows)])


def factor_rows(work, factor_ref, inverse_t_ref, base):
    halves = range(work.shape[1] // 128)
    lane = lax.broadcasted_iota(jnp.int32, (STEP, 128), 1)
    sub = lax.broadcasted_iota(jnp.int32, (STEP, 128), 0)
    steps = range(STEP)
    count = BLOCK // STEP
    rows = [
        [work[base + STEP * i : base + STEP * (i + 1), 128 * h : 128 * (h + 1)] for h in halves]
        for i in range(count)
    ]
    for g in range(count):
        j = base + STEP * g
        home, first = divmod(j, 128)
        columns = [
            [pick(rows[i][home], first + s) for s in steps]
            for i in range(g, count)
        ]
        block = [[spread(columns[0][s][r : r + 1, :]) for s in range(r + 1)] for r in steps]
        pivots, recips, inv = pivot_block(block)
        own = [[spread(rows[g][h][t : t + 1, :]) for t in steps] for h in halves]

        down = [stack(sub, [inv[t][s] if t > s else float(t == s) for t in steps]) for s in steps]
        across = [stack(sub, [inv[r][s] if r > s else float(r == s) for s in steps]) for r in steps]
        root = lax.rsqrt(stack(sub, pivots))
        corner = jnp.zeros((STEP, 128), jnp.float32)
        for s in steps:
            corner = jnp.where(lane == first + s, down[s], corner)
        solved = [weighted(down, own[h]) for h in halves]
        for h in halves:
            col = lane + 128 * h
            place = (slice(j, j + STEP), slice(128 * h, 128 * (h + 1)))
            edge = corner * root if h == home else 0.0
            factor_ref[place] = jnp.where(col >= j + sub, solved[h] * root, 0.0)
            inverse_t_ref[place] = jnp.where(col < j, solved[h] * root, edge)

        if g + 1 < count:
            inside = (lane >= first) & (lane < first + STEP)
            unit = jnp.where(lane == first + sub, 1.0, 0.0)
            across = [across[r] * recips[r] for r in steps]
            for h in halves:
                full = jnp.where(inside, corner, solved[h]) if h == home else solved[h]
                pull = weighted(across, [spread(full[t : t + 1, :]) for t in steps])
                if h == home:
                    pull = pull + unit
                pulls = [spread(pull[s : s + 1, :]) for s in steps]
                for i in range(g + 1, count):
                    rows[i][h] = rows[i][h] - weighted(columns[i - g], pulls)


def factor_kernel(own_ref, other_ref, factor_ref, inverse_t_ref, work):
    order = factor_ref.shape[0]
    half = order // 2
    first = lax.rem(lax.axis_index("col"), 2) == 0
    own, other = own_ref[...], other_ref[...]
    packed = jnp.where(first, own, other)
    corner = jnp.where(first, other, own)[:half, :]
    square = packed[:half, :]
    flipped = square.T
    row = lax.broadcasted_iota(jnp.int32, (half, half), 0)
    col = lax.broadcasted_iota(jnp.int32, (half, half), 1)
    damping = jnp.where(row == col, damping_total, 0.0)
    work[:half, :half] = jnp.where(row <= col, square, flipped) + damping
    work[:half, half:] = corner
    work[half:, :half] = corner.T
    last = jnp.where(row == col, packed[half : half + 1, :], jnp.where(row > col, square, flipped))
    work[half:, half:] = last + damping
    for base in range(0, order, BLOCK):
        end = base + BLOCK
        factor_rows(work, factor_ref, inverse_t_ref, base)
        if end < order:
            lane = lax.broadcasted_iota(jnp.int32, (1, order), 1)
            upper = factor_ref[base:end, :]
            rest = jnp.where((lane >= base) & (lane < end), 0.0, work[end:, :])
            work[end:, :] = rest - lax.dot_general(
                upper[:, end:],
                jnp.where(lane < end, inverse_t_ref[base:end, :], upper),
                (((0,), (0,)), ((), ())),
                precision=HIGHEST,
                preferred_element_type=jnp.float32,
            )


def cholesky_pair(own, other):
    order = 2 * own.shape[1]
    out = jax.ShapeDtypeStruct((order, order), jnp.float32)
    return pl.pallas_call(
        factor_kernel,
        out_shape=[out, out],
        in_specs=[VMEM] * 2,
        out_specs=[VMEM] * 2,
        scratch_shapes=[pltpu.VMEM((order, order), jnp.float32)],
        cost_estimate=pl.CostEstimate(
            flops=8 * order**3, bytes_accessed=48 * order * order, transcendentals=order
        ),
        compiler_params=PARAMS,
        name="factor",
    )(own, other)


def gram_kernel(count, panel_ref, out_ref, turned_ref):
    half = out_ref.shape[1]
    rows = panel_ref.shape[0] // count
    grams = []
    for k in range(count):
        part = panel_ref[rows * k : rows * (k + 1), :]
        turned = part.T
        turned_ref[:, rows * k : rows * (k + 1)] = turned
        grams.append(jnp.dot(turned, part, preferred_element_type=jnp.float32))
    gram = tree_sum(grams)
    row = lax.broadcasted_iota(jnp.int32, (half, half), 0)
    col = lax.broadcasted_iota(jnp.int32, (half, half), 1)
    last = gram[half:, half:]
    packed = jnp.where(row <= col, gram[:half, :half], last)
    first = lax.rem(lax.axis_index("col"), 2) == 0
    out_ref[:half, :] = jnp.where(first, packed, gram[:half, half:])
    diagonal = jnp.sum(jnp.where(row == col, last, 0.0), axis=0, keepdims=True)
    out_ref[half:, :] = jnp.broadcast_to(diagonal, (8, half))


def gram_part(count, panel):
    rows, order = panel.shape
    half = order // 2
    return pl.pallas_call(
        functools.partial(gram_kernel, count),
        out_shape=[
            jax.ShapeDtypeStruct((half + 8, half), jnp.float32),
            jax.ShapeDtypeStruct((order, rows), panel.dtype),
        ],
        in_specs=[VMEM],
        out_specs=[VMEM] * 2,
        compiler_params=PARAMS,
        name="gram_part",
    )(panel)


def cross_kernel(near, far, turned_ref, *refs):
    tiles, outs, whole = refs[:near], refs[near : near + far], refs[near + far]
    index = lax.div(lax.axis_index("row"), near)
    width = outs[0].shape[1]
    rows = tiles[0].shape[0]
    total = None
    for k, ref in enumerate(tiles):
        term = jnp.dot(
            turned_ref[:, rows * k : rows * (k + 1)], ref[...], preferred_element_type=jnp.float32
        )
        total = term if total is None else total + term
    whole[...] = total
    for k in range(far):
        start = pl.multiple_of((index ^ k) * width, width)
        outs[k][...] = whole[:, pl.ds(start, width)]


def cross_part(groups, turned, tiles):
    order = turned.shape[0]
    width = tiles[0].shape[1] // groups.far
    if width % 128:
        whole = jnp.dot(
            turned, jnp.concatenate(tiles, 0), preferred_element_type=jnp.float32
        )
        return [
            lax.dynamic_slice_in_dim(whole, (groups.far_index() ^ k) * width, width, 1)
            for k in range(groups.far)
        ]
    return pl.pallas_call(
        functools.partial(cross_kernel, groups.near, groups.far),
        out_shape=[jax.ShapeDtypeStruct((order, width), jnp.float32)] * groups.far,
        in_specs=[VMEM] * (1 + groups.near),
        out_specs=[VMEM] * groups.far,
        scratch_shapes=[pltpu.VMEM((order, tiles[0].shape[1]), jnp.float32)],
        compiler_params=PARAMS,
        name="cross_part",
    )(turned, *tiles)


def chunk_kernel(near, mask_hbm, trailing_hbm, *refs):
    outs, (mask, held, sems) = refs[:near], refs[near:]
    index = lax.rem(lax.axis_index("row"), near)
    rows, width = outs[0].shape
    first = pltpu.make_async_copy(mask_hbm, mask, sems.at[near])
    first.start()
    copies = []
    for k in [*range(1, near), 0]:
        cols = pl.ds(pl.multiple_of((index ^ k) * width, width), width)
        copies.append(pltpu.make_async_copy(trailing_hbm.at[:, cols], held.at[k], sems.at[k]))
        copies[-1].start()
    first.wait()
    for k, copy in zip([*range(1, near), 0], copies):
        copy.wait()
        for i in range(rows // TILE):
            for j in range(width // TILE):
                place = (slice(i * TILE, (i + 1) * TILE), slice(j * TILE, (j + 1) * TILE))
                tile = held[(k, *place)]
                present = mask[i, (index ^ k) * (width // TILE) + j] != 0
                outs[k][place] = jnp.where(present, tile, jnp.zeros_like(tile))


def masked_chunks(groups, trailing, tile_mask):
    rows, cols = trailing.shape
    width = cols // groups.near
    out = jax.ShapeDtypeStruct((rows, width), trailing.dtype)
    return pl.pallas_call(
        functools.partial(chunk_kernel, groups.near),
        out_shape=[out] * groups.near,
        in_specs=[pl.BlockSpec(memory_space=pltpu.HBM)] * 2,
        out_specs=[VMEM] * groups.near,
        scratch_shapes=[
            pltpu.SMEM(tile_mask.shape, tile_mask.dtype),
            pltpu.VMEM((groups.near, rows, width), trailing.dtype),
            pltpu.SemaphoreType.DMA((groups.near + 1,)),
        ],
        compiler_params=PARAMS,
        name="chunks",
    )(
        pltpu.with_memory_space_constraint(tile_mask, pltpu.HBM),
        pltpu.with_memory_space_constraint(trailing, pltpu.HBM),
    )


def update_kernel(near, far, held, basis_ref, *refs):
    count = len(held)
    chunks, parts = refs[:count], refs[count : 2 * count]
    coupling_ref, updated_ref, work, sems = refs[-4:]
    index = lax.axis_index("row")
    near_index, far_index = lax.rem(index, near), lax.div(index, near)
    copies = []

    def send(source, target, cols):
        copy = pltpu.make_async_copy(source, target.at[:, cols], sems.at[len(copies)])
        copy.start()
        copies.append(copy)

    place = 0
    for (offset, slots), chunk, part in zip(held, chunks, parts):
        width = part.shape[1] // len(slots)
        removed = jnp.dot(basis_ref[...], part[...], preferred_element_type=jnp.float32)
        for k, slot in enumerate(slots):
            inner = (far_index ^ slot) * width
            left = chunk[:, pl.ds(pl.multiple_of(inner, width), width)].astype(jnp.float32)
            result = left - removed[:, k * width : (k + 1) * width]
            work[:, place : place + width] = result.astype(work.dtype)
            start = (near_index ^ offset) * far * width + inner
            cols = pl.ds(pl.multiple_of(start, width), width)
            send(work.at[:, place : place + width], updated_ref, cols)
            send(part.at[:, k * width : (k + 1) * width], coupling_ref, cols)
            place += width
    for copy in copies:
        copy.wait()


def update_part(groups, basis, chunks, held, parts, outs):
    near, far = groups.near, groups.far
    rows, chunk = chunks[0].shape
    cols = chunk * near
    pieces = sum(len(slots) for _, slots in held)
    dtype = chunks[0].dtype
    count = 1 + 2 * len(held)
    hbm = pl.BlockSpec(memory_space=pltpu.HBM)
    return pl.pallas_call(
        functools.partial(update_kernel, near, far, held),
        out_shape=[
            jax.ShapeDtypeStruct((parts[0].shape[0], cols), dtype),
            jax.ShapeDtypeStruct((rows, cols), dtype),
        ],
        in_specs=[VMEM] * count + [hbm] * len(outs),
        out_specs=[hbm] * 2,
        input_output_aliases={count + i: i for i in range(len(outs))},
        scratch_shapes=[
            pltpu.VMEM((rows, pieces * (chunk // far)), dtype),
            pltpu.SemaphoreType.DMA((2 * pieces,)),
        ],
        compiler_params=PARAMS,
        cost_estimate=pl.CostEstimate(
            flops=2 * rows * parts[0].shape[0] * pieces * (chunk // far),
            bytes_accessed=16 * rows * pieces * (chunk // far),
            transcendentals=0,
        ),
        name="update",
    )(basis, *[chunks[offset] for offset, _ in held], *parts, *outs)


def update(groups, basis, chunks, firsts, rests):
    near = groups.near
    if (chunks[0].shape[1] // groups.far) % 128:
        return update_plain(groups, basis, chunks, firsts, rests)
    early, late = far_slots(groups)
    held = [(0, early), (0, late)] + [(i, early) for i in range(1, near)]
    outs = update_part(groups, basis, chunks, held, [firsts[0], rests[0], *firsts[1:]], [])
    held = [(i, late) for i in range(1, near)]
    return update_part(groups, basis, chunks, held, rests[1:], outs)


def update_plain(groups, basis, chunks, firsts, rests):
    near, far = groups.near, groups.far
    rows, chunk = chunks[0].shape
    width = chunk // far
    early, late = far_slots(groups)
    coupling = jnp.zeros((firsts[0].shape[0], chunk * near), firsts[0].dtype)
    masked = jnp.zeros((rows, chunk * near), chunks[0].dtype)
    for i in range(near):
        base = (groups.near_index() ^ i) * chunk
        masked = lax.dynamic_update_slice_in_dim(masked, chunks[i], base, 1)
        slots = jnp.concatenate([firsts[i], rests[i]], axis=1)
        for k, slot in enumerate([*early, *late]):
            start = base + (groups.far_index() ^ slot) * width
            part = slots[:, k * width : (k + 1) * width]
            coupling = lax.dynamic_update_slice_in_dim(coupling, part, start, 1)
    removed = jnp.dot(basis, coupling, preferred_element_type=jnp.float32)
    return coupling, (masked.astype(jnp.float32) - removed).astype(masked.dtype)


def far_slots(groups):
    return [0], list(range(1, groups.far))


def gather_slots(groups, shard):
    near = range(1, groups.near)
    rest = [groups.far_swap(shard, k) for k in range(1, groups.far)]
    rest[1], later = lax.optimization_barrier((rest[1], shard))
    firsts = [shard] + [groups.near_swap(later, k) for k in near]
    rest = jnp.concatenate(rest, axis=1)
    return firsts, [rest] + [groups.near_swap(rest, k) for k in near]


def local(groups, panel, trailing, tile_mask):
    near, far = groups.near, groups.far
    stacked = jnp.concatenate(
        [panel] + [groups.near_swap(panel, k) for k in range(1, near)], axis=0
    )
    gathered = lax.all_gather(stacked, "col", axis=1, tiled=True)

    chunks = masked_chunks(groups, trailing, tile_mask)
    tiles = [chunks[0]] + [groups.near_swap(chunks[k], k) for k in range(1, near)]

    gram_terms, turned = gram_part(near, gathered)
    gram_own = tree_sum(
        [gram_terms] + [groups.far_swap(gram_terms, k) for k in range(1, far)]
    )
    gram_other = lax.ppermute(gram_own, "col", [(i, i ^ 1) for i in range(groups.cols)])

    cross_terms = cross_part(groups, turned, tiles)
    summed = tree_sum(
        [cross_terms[0]] + [groups.far_swap(cross_terms[k], k) for k in range(1, far)]
    )

    upper_factor, inverse_t = cholesky_pair(gram_own, gram_other)
    shard = jnp.dot(inverse_t, summed, precision=HIGHEST).astype(jnp.bfloat16)
    firsts, rests = gather_slots(groups, shard)
    rows = gathered[: panel.shape[0], :].astype(jnp.float32)
    basis = lax.dot_general(
        rows, inverse_t, (((1,), (1,)), ((), ())), precision=HIGHEST
    ).astype(jnp.bfloat16)
    coupling, updated = update(groups, basis, chunks, firsts, rests)
    return (upper_factor, coupling, updated)


def solution(mesh):
    placed = (P("row", "col"), P("row", "col"), P("row", "col"))
    groups = Groups(mesh.shape["row"], mesh.shape["col"])
    return jax.shard_map(
        functools.partial(local, groups),
        mesh=mesh,
        in_specs=placed,
        out_specs=(P(), P(None, "col"), P("row", "col")),
        check_vma=False,
    )
```
